32 devices in a mesh: loop: 8 (over z, core), red: 4 (over y, x).
Axes of the slice: x: 2, y: 2, z: 4, core: 2. Of those that a mesh axis runs over, the one named last changes fastest.
Arguments:
- query_ids: int32 [512], replicated, may hold values from 0 to 8191
- layer_index: int32 [1], replicated, may hold values from 0 to 3
- gradient: bfloat16 [8192, 28672], P('loop', 'red'), may hold values from -6 to 6
- out_basis: bfloat16 [8192, 8192], P('loop'), may hold values from -0.0625 to 0.0625
- in_basis: bfloat16 [28672, 28672], P('red', 'loop'), may hold values from -0.03125 to 0.03125
- out_eigen: float32 [4, 8192], replicated, may hold values from 0.2 to 2
- in_eigen: float32 [4, 28672], P(None, 'loop'), may hold values from 0.2 to 2
Outputs:
- preconditioned: bfloat16 [512, 28672], P('loop', 'red')
The draws below stay inside these ranges and needn't reach their ends.
All inputs are finite; a program needn't handle non-finite values.
Results may differ from the reference program's by a relative error of at most 0.0055.
Values may be sent and summed in bfloat16 or wider, within the bound.
A program may use at most 192 MiB of HBM per device.

```python
import math
import jax
import jax.numpy as jnp
from jax import lax

D = 8192
FF = 28672
QUERIES = 512
LAYERS = 4


def place_ends(values, rng, low, largest):
    dims = values.shape
    index_at = [jax.random.randint(jax.random.fold_in(rng, axis), (), 0, dims[axis]) for axis in range(len(dims))]
    values = values.at[tuple(index_at)].set(low)
    longest = dims.index(max(dims))
    index_at[longest] = (index_at[longest] + 1) % dims[longest]
    return values.at[tuple(index_at)].set(largest)


def steps_of(key, dims, split, low, largest):
    level, own = 1.0, jax.random.fold_in(key, 6)
    for position, shards_of in split:
        heights = jnp.exp(jax.random.uniform(jax.random.fold_in(own, position), (shards_of,), jnp.float32, low / len(split), largest / len(split)))
        level = level * jnp.repeat(heights, dims[position] // shards_of).reshape([-1 if axis == position else 1 for axis in range(len(dims))])
    return level


def centred(key, shape, spread, most, cuts=(), dtype=jnp.bfloat16):
    values = jax.random.normal(key, shape, jnp.float32) * spread
    if len(cuts) > 0:
        values = steps_of(key, shape, cuts, -0.22, 0.18) * values
    return jnp.clip(values, min=-most, max=most).astype(dtype)


def setup_inputs(seed: int = 0) -> dict:
    splits = jax.random.split(jax.random.key(seed), 8)
    return {
        "query_ids": place_ends(jax.random.randint(splits[0], (QUERIES,), 0, D), jax.random.fold_in(splits[0], 1), 0, D - 1).astype(jnp.int32),
        "layer_index": jax.random.randint(splits[1], (1,), 0, LAYERS).astype(jnp.int32),
        "gradient": centred(splits[2], (D, FF), 1.0, 6.0, ((0, 8), (1, 4))),
        "out_basis": centred(splits[3], (D, D), D ** -0.5, 0.0625, ((0, 8),)),
        "in_basis": centred(splits[4], (FF, FF), FF ** -0.5, 0.03125, ((0, 4), (1, 8))),
        "out_eigen": jnp.clip(jnp.exp(jax.random.uniform(splits[5], (LAYERS, D), jnp.float32, math.log(0.2), math.log(2.0))), 0.2, 2.0),
        "in_eigen": jnp.clip(jnp.exp(math.log(2.0) - 2.3025851 * jax.random.uniform(splits[6], (LAYERS, FF), jnp.float32) ** steps_of(splits[6], (LAYERS, FF), ((1, 8),), -0.2, 0.2)), 0.2, 2.0),
    }


damping = 0.05


def reference(query_ids, layer_index, gradient, out_basis, in_basis, out_eigen, in_eigen):
    selected = jnp.take(out_basis, query_ids, axis=1)
    rows_w = lax.dot_general(selected, gradient, (((0,), (0,)), ((), ())), preferred_element_type=jnp.float32).astype(jnp.bfloat16)
    rotated = jnp.dot(rows_w, in_basis, preferred_element_type=jnp.float32)
    eigen_rows = jnp.take(jnp.take(out_eigen, layer_index, axis=0)[0], query_ids)
    eigen_cols = jnp.take(in_eigen, layer_index, axis=0)[0]
    scaled = (rotated / (eigen_rows[:, None] * eigen_cols[None, :] + damping)).astype(jnp.bfloat16)
    result = lax.dot_general(scaled, in_basis, (((1,), (1,)), ((), ())), preferred_element_type=jnp.float32)
    return result.astype(jnp.bfloat16)
```

```python
import jax
import jax.numpy as jnp
from jax import lax
from jax.sharding import PartitionSpec as P

damping = 0.05
QUERY_CHUNKS = 2
COLUMN_CHUNKS = 2
RED_CHUNKS = 2
OUT_CHUNKS = 2


def pieces(size, count):
    while size % count or (size // count) % 128:
        count -= 1
    return [(k * (size // count), size // count) for k in range(count)]


def make(mesh):
    loop, red = mesh.shape["loop"], mesh.shape["red"]
    chips = loop // 2
    half = chips // 2
    f32, bf16 = jnp.float32, jnp.bfloat16

    def both(pairs):
        return [(2 * a + c, 2 * b + c) for a, b in pairs for c in range(2)]

    def send(x, pairs):
        return lax.ppermute(x.astype(bf16), "loop", both(pairs))

    def swap_cores(x):
        return lax.ppermute(x.astype(bf16), "loop", [(i, i ^ 1) for i in range(loop)])

    def inward(i):
        return [(i, i + 1), (chips - 1 - i, chips - 2 - i)]

    def outward(i):
        return [(b, a) for a, b in inward(i)]

    middle = [(half - 1, half), (half, half - 1)]

    def line_sum(x, chip):
        for i in range(half - 1):
            x = x + send(x, inward(i)).astype(f32)
        x = x + send(x, middle).astype(f32)
        x = x.astype(bf16)
        for i in reversed(range(half - 1)):
            took = send(x, outward(i))
            x = jnp.where((chip == i) | (chip == chips - 1 - i), took, x)
        return x

    def line_scatter(x, chip):
        left = chip < half

        def cut(x, start, count):
            return lax.dynamic_slice_in_dim(x, start, count, 0)

        def add(x, took, start):
            here = cut(x, start, took.shape[0]) + took.astype(f32)
            return lax.dynamic_update_slice_in_dim(x, here, start, 0)

        for i in range(half - 1):
            at = jnp.where(left, i + 1, 0)
            x = add(x, send(cut(x, at, chips - 1 - i), inward(i)), at)
        took = send(cut(x, jnp.where(left, half, 0), half), middle)
        at = jnp.where(left, 0, half)
        x = cut(x, at, half) + took.astype(f32)
        for i in reversed(range(half - 1)):
            first = jnp.where(left, 0, half - 1 - i)
            x = add(x, send(cut(x, first, i + 1), outward(i)), first)
        return cut(x, chip - at, 1)[0]

    def red_sum(x, turn):
        bits = [1 << b for b in range(red.bit_length() - 1)]
        for k in range(len(bits)):
            bit = bits[(k + turn) % len(bits)]
            took = lax.ppermute(x.astype(bf16), "red", [(i, i ^ bit) for i in range(red)])
            x = x + took.astype(f32)
        return x

    def per_device(query_ids, layer_index, gradient, out_basis, in_basis, out_eigen, in_eigen):
        me = lax.axis_index("loop")
        chip, core = me // 2, me % 2
        queries = query_ids.shape[0]
        r = queries // loop // QUERY_CHUNKS
        rows, cols = in_basis.shape
        ids = query_ids.reshape(chips, 2, QUERY_CHUNKS, r).transpose(2, 1, 0, 3)
        ids = jnp.where(core == 0, ids, ids[:, ::-1]).reshape(QUERY_CHUNKS, -1)
        out_row = lax.dynamic_index_in_dim(out_eigen, layer_index[0], 0, keepdims=False)
        eigen_cols = lax.dynamic_index_in_dim(in_eigen, layer_index[0], 0, keepdims=False)
        every = lax.broadcasted_iota(jnp.int32, (queries, out_basis.shape[1]), 1)
        pick = (ids.reshape(-1)[:, None] == every).astype(bf16)
        selected = lax.dot_general(
            pick, out_basis, (((1,), (1,)), ((), ())), preferred_element_type=f32
        ).astype(bf16)
        eigen_rows = jnp.take(out_row, ids.reshape(-1))
        per = queries // QUERY_CHUNKS
        own = per // 2
        outs = []
        for j in range(QUERY_CHUNKS):
            chosen = selected[j * per : (j + 1) * per]
            rot = None
            for at, size in pieces(rows, COLUMN_CHUNKS):
                part = jnp.dot(chosen, gradient[:, at : at + size], preferred_element_type=f32)
                mine = part[:own] + swap_cores(part[own:]).astype(f32)
                mine = line_sum(mine, chip)
                rows_w = jnp.concatenate([mine, swap_cores(mine)], axis=0)
                term = jnp.dot(rows_w, in_basis[at : at + size], preferred_element_type=f32)
                rot = term if rot is None else rot + term
            scaled = []
            level = eigen_rows[j * per : (j + 1) * per, None]
            for turn, (at, size) in enumerate(pieces(cols, RED_CHUNKS)):
                total = red_sum(rot[:, at : at + size], turn)
                scale = level * eigen_cols[None, at : at + size] + damping
                scaled.append((total / scale).astype(bf16))
            scaled = jnp.concatenate(scaled, axis=1)
            done = []
            for at, size in pieces(rows, OUT_CHUNKS):
                part = lax.dot_general(
                    scaled, in_basis[at : at + size], (((1,), (1,)), ((), ())),
                    preferred_element_type=f32,
                )
                mine = part[:own] + swap_cores(part[own:]).astype(f32)
                done.append(line_scatter(mine.reshape(chips, r, size), chip).astype(bf16))
            outs.append(jnp.concatenate(done, axis=1))
        return jnp.concatenate(outs, axis=0)

    return per_device


def solution(mesh):
    return jax.shard_map(
        make(mesh),
        mesh=mesh,
        in_specs=(
            P(),
            P(),
            P("loop", "red"),
            P("loop", None),
            P("red", "loop"),
            P(),
            P(None, "loop"),
        ),
        out_specs=P("loop", "red"),
        check_vma=False,
    )
```

```python
import jax
import jax.numpy as jnp
from jax import lax
from jax.experimental import pallas as pl
from jax.experimental.pallas import tpu as pltpu
from jax.sharding import PartitionSpec as P

damping = 0.05
QUERY_CHUNKS = 2
ROW_PIECES = 16
RED_CHUNKS = 2
OUT_CHUNKS = 2


def pieces(size, count):
    while size % count or (size // count) % 128:
        count -= 1
    return [(k * (size // count), size // count) for k in range(count)]


def make(mesh):
    loop, red = mesh.shape["loop"], mesh.shape["red"]
    chips = loop // 2
    half = chips // 2
    f32, bf16 = jnp.float32, jnp.bfloat16

    def both(pairs):
        return [(2 * a + c, 2 * b + c) for a, b in pairs for c in range(2)]

    def send(x, pairs):
        return lax.ppermute(x.astype(bf16), "loop", both(pairs))

    def swap_cores(x):
        return lax.ppermute(x.astype(bf16), "loop", [(i, i ^ 1) for i in range(loop)])

    def inward(i):
        return [(i, i + 1), (chips - 1 - i, chips - 2 - i)]

    def outward(i):
        return [(b, a) for a, b in inward(i)]

    middle = [(half - 1, half), (half, half - 1)]

    def line_sum_kernel(
        mine, other, out, swapped, arrived, crossed, sent, acc,
        swap_s, swap_r, in_s, in_r, mid_s, mid_r, out_s, out_r, back_s, back_r,
    ):
        me = lax.axis_index("loop")
        chip, core = me // 2, me % 2
        left = chip < half
        is_mid = (chip == half - 1) | (chip == half)
        is_end = (chip == 0) | (chip == chips - 1)
        partner = chip * 2 + 1 - core
        inner = jnp.where(left, me + 2, me - 2)
        outer = jnp.where(left, me - 2, me + 2)
        own = mine.shape[0]
        step = own // ROW_PIECES

        def at(ref, k, base=0):
            return ref.at[pl.ds(pl.multiple_of(base + k * step, step), step)]

        def remote(src, dst, s, r, k, to):
            return pltpu.make_async_remote_copy(
                src_ref=src, dst_ref=dst, send_sem=s.at[k], recv_sem=r.at[k],
                device_id={"loop": to}, device_id_type=pl.DeviceIdType.MESH,
            )

        def swap(k):
            return remote(at(other, k), at(swapped, k), swap_s, swap_r, k, partner)

        def go_in(k):
            return remote(at(sent, k), at(arrived, k), in_s, in_r, k, inner)

        def go_mid(k):
            return remote(at(sent, k), at(crossed, k), mid_s, mid_r, k, inner)

        def go_out(k):
            return remote(at(out, k), at(out, k), out_s, out_r, k, outer)

        def go_back(k):
            return remote(at(out, k), at(out, k, own), back_s, back_r, k, partner)

        barrier = pltpu.get_barrier_semaphore()

        def greet(to):
            pl.semaphore_signal(
                barrier, inc=1, device_id={"loop": to}, device_id_type=pl.DeviceIdType.MESH
            )

        greet(partner)
        greet(inner)

        @pl.when(jnp.logical_not(is_end))
        def _():
            greet(outer)
            pl.semaphore_wait(barrier, 3)

        @pl.when(is_end)
        def _():
            pl.semaphore_wait(barrier, 2)

        def every(f):
            lax.fori_loop(0, ROW_PIECES, lambda k, c: (f(k), c)[1], 0)

        def first(k):
            swap(k).wait_recv()
            rows = pl.ds(pl.multiple_of(k * step, step), step)
            sent[rows] = (mine[rows] + swapped[rows].astype(f32)).astype(bf16)

            @pl.when(jnp.logical_not(is_end))
            def _():
                go_in(k).wait_recv()
                acc[rows] = mine[rows] + swapped[rows].astype(f32) + arrived[rows].astype(f32)
                sent[rows] = acc[rows].astype(bf16)

            @pl.when(is_mid)
            def _():
                go_mid(k).start()

            @pl.when(jnp.logical_not(is_mid))
            def _():
                go_in(k).start()

        def last(k):
            rows = pl.ds(pl.multiple_of(k * step, step), step)

            @pl.when(is_mid)
            def _():
                go_mid(k).wait_recv()
                out[rows] = (acc[rows] + crossed[rows].astype(f32)).astype(bf16)

            @pl.when(jnp.logical_not(is_mid))
            def _():
                go_out(k).wait_recv()

            @pl.when(jnp.logical_not(is_end))
            def _():
                go_out(k).start()

            go_back(k).start()

        every(lambda k: swap(k).start())

        def main(k):
            first(k)

            @pl.when(is_mid & (k >= 2))
            def _():
                last(k - 2)

        every(main)
        begin = jnp.where(is_mid, ROW_PIECES - 2, 0)
        lax.fori_loop(begin, ROW_PIECES, lambda k, c: (last(k), c)[1], 0)

        def drain(k):
            swap(k).wait_send()
            go_back(k).wait()

            @pl.when(is_mid)
            def _():
                go_mid(k).wait_send()

            @pl.when(jnp.logical_not(is_mid))
            def _():
                go_in(k).wait_send()

            @pl.when(jnp.logical_not(is_end))
            def _():
                go_out(k).wait_send()

        every(drain)

    def line_sum(mine, other):
        own, cols = mine.shape
        vmem = pl.BlockSpec(memory_space=pltpu.VMEM)
        sems = pltpu.SemaphoreType.DMA((ROW_PIECES,))
        return pl.pallas_call(
            line_sum_kernel,
            out_shape=jax.ShapeDtypeStruct((2 * own, cols), bf16),
            in_specs=[vmem] * 2,
            out_specs=vmem,
            scratch_shapes=[pltpu.VMEM((own, cols), bf16)] * 4
            + [pltpu.VMEM((own, cols), f32)]
            + [sems] * 10,
            compiler_params=pltpu.CompilerParams(
                collective_id=0, has_side_effects=True, vmem_limit_bytes=60 * 1024 * 1024
            ),
        )(mine, other)

    def line_scatter(x, chip):
        left = chip < half

        def cut(x, start, count):
            return lax.dynamic_slice_in_dim(x, start, count, 0)

        def add(x, took, start):
            here = cut(x, start, took.shape[0]) + took.astype(f32)
            return lax.dynamic_update_slice_in_dim(x, here, start, 0)

        for i in range(half - 1):
            at = jnp.where(left, i + 1, 0)
            x = yield add(x, send(cut(x, at, chips - 1 - i), inward(i)), at)
        took = send(cut(x, jnp.where(left, half, 0), half), middle)
        at = jnp.where(left, 0, half)
        x = yield cut(x, at, half) + took.astype(f32)
        for i in reversed(range(half - 1)):
            first = jnp.where(left, 0, half - 1 - i)
            x = yield add(x, send(cut(x, first, i + 1), outward(i)), first)
        return cut(x, chip - at, 1)[0]

    def red_step(x, k):
        bits = [1 << b for b in range(red.bit_length() - 1)]
        bit = bits[k % len(bits)]
        took = lax.ppermute(x.astype(bf16), "red", [(i, i ^ bit) for i in range(red)])
        return x + took.astype(f32)

    red_steps = red.bit_length() - 1

    def per_device(query_ids, layer_index, gradient, out_basis, in_basis, out_eigen, in_eigen):
        me = lax.axis_index("loop")
        chip, core = me // 2, me % 2
        queries = query_ids.shape[0]
        r = queries // loop // QUERY_CHUNKS
        rows, cols = in_basis.shape
        ids = query_ids.reshape(chips, 2, QUERY_CHUNKS, r).transpose(2, 1, 0, 3)
        ids = jnp.where(core == 0, ids, ids[:, ::-1]).reshape(QUERY_CHUNKS, -1)
        out_row = lax.dynamic_index_in_dim(out_eigen, layer_index[0], 0, keepdims=False)
        eigen_cols = lax.dynamic_index_in_dim(in_eigen, layer_index[0], 0, keepdims=False)
        eigen_rows = jnp.take(out_row, ids.reshape(-1)).reshape(QUERY_CHUNKS, -1)
        per = queries // QUERY_CHUNKS
        own = per // 2
        red_pieces = pieces(cols, RED_CHUNKS)
        out_pieces = pieces(rows, OUT_CHUNKS)
        rot, scaled, outs = {}, {}, {}

        every = lax.broadcasted_iota(jnp.int32, (queries, out_basis.shape[1]), 1)
        order = jnp.concatenate([ids[:, :own].reshape(-1), ids[:, own:].reshape(-1)])
        selected = lax.dot_general(
            (order[:, None] == every).astype(bf16), out_basis,
            (((1,), (1,)), ((), ())), preferred_element_type=f32,
        ).astype(bf16)
        mine = jnp.dot(selected[: queries // 2], gradient, preferred_element_type=f32)
        other = jnp.dot(selected[queries // 2 :], gradient, preferred_element_type=f32)
        rows_w = line_sum(mine, other.astype(bf16)).reshape(2, QUERY_CHUNKS, own, rows)

        def rotate(j):
            here = rows_w[:, j].reshape(per, rows)
            rot[j] = jnp.dot(here, in_basis, preferred_element_type=f32)
            return
            yield

        def red_job(j):
            whole = rot.pop(j)
            parts = [whole[:, at : at + size] for at, size in red_pieces]
            for first in range(0, len(parts), 2):
                for k in range(red_steps):
                    for turn in range(first, min(first + 2, len(parts))):
                        parts[turn] = red_step(parts[turn], k + turn)
                    if k == red_steps - 1:
                        for turn in range(first, min(first + 2, len(parts))):
                            at, size = red_pieces[turn]
                            scale = eigen_rows[j][:, None] * eigen_cols[None, at : at + size]
                            parts[turn] = (parts[turn] / (scale + damping)).astype(bf16)
                    if k < red_steps - 1 or first + 2 < len(parts):
                        parts = yield parts
            scaled[j] = jnp.concatenate(parts, axis=1)

        def out_job(j, n, at, size):
            part = lax.dot_general(
                scaled[j], in_basis[at : at + size], (((1,), (1,)), ((), ())),
                preferred_element_type=f32,
            )
            mine = yield part[:own] + swap_cores(part[own:]).astype(f32)
            done = yield from line_scatter(mine.reshape(chips, r, size), chip)
            outs[j, n] = done.astype(bf16)

        gathers = [rotate(j) for j in range(QUERY_CHUNKS)]
        reds = list(range(QUERY_CHUNKS))
        scatters = [
            (j, n, at, size)
            for j in range(QUERY_CHUNKS) for n, (at, size) in enumerate(out_pieces)
        ]
        running = []
        while gathers or reds or scatters or running:
            if gathers:
                running.append([gathers.pop(0), None])
            if reds and reds[0] in rot:
                running.append([red_job(reds.pop(0)), None])
            if scatters and scatters[0][0] in scaled:
                running.append([out_job(*scatters.pop(0)), None])
            going = []
            for job, value in running:
                try:
                    going.append([job, job.send(value)])
                except StopIteration:
                    pass
            running = going
            values = ([v for _, v in running], rot, scaled, outs)
            values = lax.optimization_barrier(values)
            running = [[job, v] for (job, _), v in zip(running, values[0])]
            for kept, new in zip((rot, scaled, outs), values[1:]):
                kept.update(new)
        return jnp.concatenate(
            [
                jnp.concatenate([outs[j, n] for n in range(len(out_pieces))], axis=1)
                for j in range(QUERY_CHUNKS)
            ],
            axis=0,
        )

    return per_device


def solution(mesh):
    return jax.shard_map(
        make(mesh),
        mesh=mesh,
        in_specs=(
            P(),
            P(),
            P("loop", "red"),
            P("loop", None),
            P("red", "loop"),
            P(),
            P(None, "loop"),
        ),
        out_specs=P("loop", "red"),
        check_vma=False,
    )
```
